256 devices in a mesh: req: 64 (over x, z, core), tp: 4 (over y).
Axes of the slice: x: 4, y: 4, z: 8, core: 2. Of those that a mesh axis runs over, the one named last changes fastest.
Arguments:
- queries: bfloat16 [512, 2560], P('req', 'tp'), may hold values from -68 to 68, as said below
- new_kv: bfloat16 [512, 4, 256], P('req', 'tp'), may hold values from -6 to 6
- residual: bfloat16 [512, 2560], P('req', 'tp'), may hold values from -6 to 6
- kv_cache: bfloat16 [512, 512, 4, 256], P('req', None, 'tp'), may hold values from -6 to 6
- cache_len: int32 [512], P('req'), may hold values from 1 to 511, as said below
- request_perm: int32 [512], replicated, may hold values from 0 to 511, each once
- expert_ids: int32 [512, 6], P('req'), may hold values from 0 to 63, all different within a row; in each aligned block of 8 rows (0 to 7, 8 to 15, ...) at most 2 rows name the same one
- route_wt: float32 [512, 6], P('req'), may hold values from 0.05 to 1
- attn_out_w: bfloat16 [2560, 2560], P('tp'), may hold values from -0.125 to 0.125
- post_gain: float32 [2560], replicated, may hold values from 0.25 to 1.75
- expert_gate_up: bfloat16 [64, 2, 2560, 1536], P('req', None, None, 'tp'), may hold values from -0.125 to 0.125
- expert_down: bfloat16 [64, 1536, 2560], P('req', 'tp'), may hold values from -0.15625 to 0.15625
- final_gain: float32 [2560], replicated, may hold values from 0.25 to 1.75
- vocab_w: bfloat16 [103424, 2560], P(('req', 'tp')), may hold values from -0.125 to 0.125
Outputs:
- hidden_out: bfloat16 [512, 2560], P('req', 'tp')
- state_norm: float32 [512], P('req')
- top_logit: float32 [512], P('req')
The draws below stay inside these ranges and needn't reach their ends.
Inputs may be any that keep to these rules, and one draw needn't show every extreme that they name: queries lie within this range. Slot s holds cache_len[s] filled rows; some slot holds exactly 511. `request_perm`: a permutation of the slots. `expert_ids`: each row names 6 different experts; among the rows of one device (aligned blocks of 8 rows) no expert is named more than 2 times, and in some block one expert is named exactly 2 times.
All inputs are finite; a program needn't handle non-finite values.
Results may differ from the reference program's by a relative error of at most 0.007.
Values may be sent and summed in bfloat16 or wider, within the bound.
No kernel may reach another device: no remote copies, remote signals or barrier semaphores. Data moves between devices by JAX's collectives and lax.ppermute only.
A program may use at most 64 MiB of HBM per device.

```python
import math
import jax
import jax.numpy as jnp
import numpy as np
from jax import lax

D = 2560
KVH = 4
HD = 128
FFE = 1536
TOPK = 6
VOC_DEV = 404
REQ_DEV = 8
CACHE = 512
QW = 2560
EXPERTS = 64
REQUESTS = 512
CAP = 2
VOCAB = 103424
N_REQ = 64


def draw_queries(key, part):
    base = jax.random.normal(key, (REQUESTS, QW), jnp.float32)
    return jnp.clip(base, -6.0, 6.0).astype(jnp.bfloat16)


def draw_cache_len(key, part):
    first_key, second_key, third_key = jax.random.split(jax.random.fold_in(key, 11), 3)
    first_len = jax.random.randint(first_key, (REQUESTS,), 1, CACHE, dtype=jnp.int32)
    second_len = jax.random.randint(second_key, (REQUESTS,), 1, CACHE, dtype=jnp.int32)
    lengths = jnp.minimum(first_len, second_len)
    longest = jax.random.randint(third_key, (), 0, REQUESTS, dtype=jnp.int32)
    return lengths.at[longest].set(CACHE - 1).astype(jnp.int32)


def level_of(key, dims, cuts, low, high):
    gain, own = 1.0, jax.random.fold_in(key, 6)
    for dim, blocks in cuts:
        draws = jnp.exp(jax.random.uniform(jax.random.fold_in(own, dim), (blocks,), jnp.float32, low / len(cuts), high / len(cuts)))
        gain = gain * jnp.repeat(draws, dims[dim] // blocks).reshape([-1 if axis == dim else 1 for axis in range(len(dims))])
    return gain


def deal_out(own_key, own, number, rows, amount, top, most, skew):
    ranking = jax.random.permutation(own_key, amount)
    heavy_load, usual = load_shares(amount, rows * top, most, skew, True), load_shares(amount, rows * top, most, skew, False)
    places = jnp.arange(amount)

    def named(tallies, rotation):
        used = int((tallies > 0).sum())
        fixed = max(1, used // 4)
        moved = fixed + (places - fixed + rotation * (used - fixed)) % max(1, amount - fixed)
        return jnp.zeros((amount,), jnp.int32).at[ranking[jnp.where(places < fixed, places, moved)]].set(jnp.asarray(tallies, jnp.int32))

    tallies = jnp.where(number % 4 == 0, named(heavy_load, number // 4), named(usual, number - number // 4 - 1))
    mixed = jax.random.permutation(jax.random.fold_in(own, 3), amount)
    donor, receiver = mixed[0:amount // 2 * 2:2], mixed[1:amount // 2 * 2:2]
    margin = jnp.minimum(tallies[donor] - 1, most - tallies[receiver]) // 2
    margin = jnp.where((donor == ranking[0]) | (receiver == ranking[0]) | (tallies[receiver] == 0), 0, jnp.maximum(margin, 0))
    moved = jax.random.randint(jax.random.fold_in(own, 4), (amount // 2,), 0, 1 << 20) % (margin + 1)
    tallies = tallies.at[donor].add(-moved).at[receiver].add(moved)
    members = jnp.searchsorted(jnp.cumsum(tallies), jnp.arange(rows * top), side="right").astype(jnp.int32)
    grid = members.reshape(top, rows).T
    grid = grid[jax.random.permutation(jax.random.fold_in(own, 1), rows)]
    rotation = jax.random.randint(jax.random.fold_in(own, 2), (rows, 1), 0, top)
    return jnp.take_along_axis(grid, (jnp.arange(top)[None, :] + rotation) % top, axis=1)


def load_shares(count, total, bound, slope, full):
    loads = [(1 << 20) // math.isqrt(standing ** slope) + 1 for standing in range(1, count + 1)]
    largest = bound if full else min(bound, max(-(-total // count), total * loads[0] // sum(loads)))
    least = 1 if total - largest >= count - 1 else 0
    holding, rest = [largest] + [least] * (count - 1), total - largest - least * (count - 1)
    while rest > 0:
        candidates = [i for i in range(1, count) if holding[i] < largest] or [i for i in range(1, count) if holding[i] < bound]
        pool, remaining = sum([loads[i] for i in candidates]), rest
        for i in candidates:
            more = min(bound - holding[i], max(1, remaining * loads[i] // pool), rest)
            holding[i] = holding[i] + more
            rest = rest - more
    return np.array(holding)


def centred(stream_key, extent, width, most, shards=(), kind=jnp.bfloat16):
    factor_of = level_of(stream_key, extent, shards, -0.22, 0.18) if shards else 1.0
    entries = jax.random.normal(stream_key, extent, jnp.float32) * width * factor_of
    return jnp.minimum(jnp.maximum(entries, -most), most).astype(kind)


def setup_inputs(seed: int = 0) -> dict:
    seeds = jax.random.split(jax.random.key(seed), 15)
    queries = draw_queries(jax.random.fold_in(seeds[14], 71), 0)
    new_kv = centred(seeds[1], (REQUESTS, KVH, 2 * HD), 1.0, 6.0, ((0, 64), (1, 4)))
    residual = centred(seeds[2], (REQUESTS, D), 1.0, 6.0, ((0, 64), (1, 4)))
    kv_cache = centred(seeds[3], (REQUESTS, CACHE, KVH, 2 * HD), 1.0, 6.0, ((0, 64), (2, 4)))
    cache_len = draw_cache_len(jax.random.fold_in(seeds[14], 71), 0)
    request_perm = jax.random.permutation(seeds[5], REQUESTS).astype(jnp.int32)
    expert_ids_keys = jax.random.split(jax.random.fold_in(seeds[6], 1), REQUESTS // REQ_DEV)
    expert_ids_turns = jax.random.permutation(jax.random.fold_in(seeds[6], 3), REQUESTS // REQ_DEV)
    expert_ids = jax.vmap(lambda own, number: deal_out(jax.random.fold_in(seeds[6], 2), own, number, REQ_DEV, EXPERTS, TOPK, CAP, 2))(expert_ids_keys, expert_ids_turns).reshape((REQUESTS, TOPK))
    route_wt = jnp.clip(jnp.exp(math.log(1.0) - 2.9957323 * jax.random.uniform(seeds[7], (REQUESTS, TOPK), jnp.float32) ** level_of(seeds[7], (REQUESTS, TOPK), ((0, 64),), -0.2, 0.2)), 0.05, 1.0)
    attn_out_w = centred(seeds[8], (QW, D), QW ** -0.5, 0.125, ((0, 4),))
    post_gain = jnp.clip(1.0 + 0.15 * jax.random.normal(seeds[9], (D,), jnp.float32), 0.25, 1.75)
    expert_gate_up = centred(seeds[10], (EXPERTS, 2, D, FFE), D ** -0.5, 0.125, ((0, 64), (3, 4)))
    expert_down = centred(seeds[11], (EXPERTS, FFE, D), FFE ** -0.5, 0.15625, ((0, 64), (1, 4)))
    final_gain = jnp.clip(1.0 + 0.15 * jax.random.normal(seeds[12], (D,), jnp.float32), 0.25, 1.75)
    vocab_w = centred(seeds[13], (VOCAB, D), D ** -0.5, 0.125, ((0, 256),))
    return {"queries": queries, "new_kv": new_kv, "residual": residual, "kv_cache": kv_cache, "cache_len": cache_len, "request_perm": request_perm, "expert_ids": expert_ids, "route_wt": route_wt, "attn_out_w": attn_out_w, "post_gain": post_gain, "expert_gate_up": expert_gate_up, "expert_down": expert_down, "final_gain": final_gain, "vocab_w": vocab_w}


epsilon = 1e-05

def attend(queries, fresh_kv, kv_block, lengths, head_dim):
    slot_count, context, kv_heads, _ = kv_block.shape
    groups = queries.shape[1] // head_dim // kv_heads
    query_heads = queries.reshape(slot_count, kv_heads, groups, head_dim).astype(jnp.float32)
    key_part = kv_block[..., :head_dim].astype(jnp.float32)
    value_part = kv_block[..., head_dim:].astype(jnp.float32)
    score_scale = head_dim ** (-0.5)
    scores = jnp.einsum('skgd,sckd->skgc', query_heads, key_part) * score_scale
    live_mask = (jnp.arange(context, dtype=jnp.int32)[None, :] < lengths[:, None])[:, None, None, :]
    scores = jnp.where(live_mask, scores, -1e+30)
    own_score = jnp.einsum('skgd,skd->skg', query_heads, fresh_kv[..., :head_dim].astype(jnp.float32)) * score_scale
    highest = jnp.maximum(lax.optimization_barrier(jnp.max(scores, axis=-1)), own_score)
    weights = jnp.where(live_mask, jnp.exp(scores - highest[..., None]), 0.0)
    own_weight = jnp.exp(own_score - highest)
    total_weight = lax.optimization_barrier(jnp.sum(weights, axis=-1)) + own_weight
    rounded = lax.optimization_barrier(weights.astype(jnp.bfloat16)).astype(jnp.float32)
    own_round = lax.optimization_barrier(own_weight.astype(jnp.bfloat16)).astype(jnp.float32)
    mixed_sum = jnp.einsum('skgc,sckd->skgd', rounded, value_part)
    mixed_sum = mixed_sum + own_round[..., None] * fresh_kv[:, :, None, head_dim:].astype(jnp.float32)
    return (mixed_sum / total_weight[..., None]).reshape(slot_count, -1).astype(jnp.bfloat16)

def expert_rows(inputs, gate_up, down_proj):
    gate_val = jnp.dot(inputs, gate_up[0], preferred_element_type=jnp.float32)
    upward = jnp.dot(inputs, gate_up[1], preferred_element_type=jnp.float32)
    active = (jax.nn.silu(gate_val) * upward).astype(jnp.bfloat16)
    return jnp.dot(active, down_proj, preferred_element_type=jnp.float32)

def rms_scale(values):
    return lax.rsqrt(lax.optimization_barrier(jnp.mean(values * values, axis=-1, keepdims=True)) + epsilon)

def reference(queries, new_kv, residual, kv_cache, cache_len, request_perm, expert_ids, route_wt, attn_out_w, post_gain, expert_gate_up, expert_down, final_gain, vocab_w):
    slot_count = REQUESTS
    inverse_order = jnp.zeros((slot_count,), jnp.int32).at[request_perm].set(jnp.arange(slot_count, dtype=jnp.int32))
    dealt_q = queries[inverse_order]
    dealt_kv = new_kv[inverse_order]
    dealt_res = residual[inverse_order]

    def block_attend(block_items):
        return attend(block_items[0], block_items[1], block_items[2], block_items[3], HD)
    attended = lax.map(block_attend, (dealt_q.reshape(N_REQ, REQ_DEV, QW), dealt_kv.reshape(N_REQ, REQ_DEV, KVH, 2 * HD), kv_cache.reshape(N_REQ, REQ_DEV, CACHE, KVH, 2 * HD), cache_len.reshape(N_REQ, REQ_DEV))).reshape(slot_count, QW)
    mixed_sum = dealt_res.astype(jnp.float32) + jnp.dot(attended, attn_out_w, preferred_element_type=jnp.float32)
    normed = (mixed_sum * rms_scale(mixed_sum) * post_gain).astype(jnp.bfloat16)
    experts = N_REQ
    hit_table = (expert_ids[..., None] == jnp.arange(experts, dtype=jnp.int32)).astype(jnp.int32)
    blocked = hit_table.reshape(N_REQ, REQ_DEV * TOPK, experts)
    earlier = jnp.cumsum(blocked, axis=1) - blocked
    slot_rank = lax.optimization_barrier(jnp.sum(earlier * blocked, axis=-1)).reshape(slot_count, TOPK)
    source = (jnp.arange(slot_count, dtype=jnp.int32) // REQ_DEV)[:, None]
    target = (expert_ids * N_REQ + source) * CAP + slot_rank
    slot_table = jnp.full((experts * N_REQ * CAP,), slot_count, jnp.int32)
    slot_table = slot_table.at[target.reshape(-1)].set(jnp.repeat(jnp.arange(slot_count, dtype=jnp.int32), TOPK))
    padded = jnp.concatenate([normed, jnp.zeros((1, D), jnp.bfloat16)], axis=0)
    inputs = padded[slot_table].reshape(experts, N_REQ * CAP, D)

    def run_expert(block_items):
        return expert_rows(block_items[0], block_items[1], block_items[2])
    outputs = lax.map(run_expert, (inputs, expert_gate_up, expert_down)).reshape(-1, D)
    route_share = route_wt / lax.optimization_barrier(jnp.sum(route_wt, axis=1, keepdims=True))
    moe = lax.optimization_barrier(jnp.sum(route_share[..., None] * outputs[target], axis=1))
    new_state = (mixed_sum + moe).astype(jnp.bfloat16)
    state_flat = new_state.astype(jnp.float32)
    hidden_out = new_state[request_perm]
    state_norm = jnp.sqrt(lax.optimization_barrier(jnp.mean(state_flat * state_flat, axis=1)) + epsilon)[request_perm]
    ready_rows = (state_flat * rms_scale(state_flat) * final_gain).astype(jnp.bfloat16)

    def block_top(vocab_block):
        logits = lax.dot_general(ready_rows, vocab_block, (((1,), (1,)), ((), ())), preferred_element_type=jnp.float32)
        return lax.optimization_barrier(jnp.max(logits, axis=1))
    block_tops = lax.map(block_top, vocab_w.reshape(-1, VOC_DEV, D))
    top_logit = lax.optimization_barrier(jnp.max(block_tops, axis=0))[request_perm]
    return (hidden_out, state_norm, top_logit)
```

```python
import jax
import jax.numpy as jnp
from jax import lax
from jax.sharding import Mesh, PartitionSpec as P

epsilon = 1e-05
X, Z, C, Y = 4, 8, 2, 4
REQ = ("x", "z", "c")
ALL = ("x", "z", "c", "y")
BF = jnp.bfloat16
F32 = jnp.float32


def attend(queries, fresh_kv, kv_block, lengths, head_dim):
    slot_count, context, kv_heads, _ = kv_block.shape
    groups = queries.shape[1] // head_dim // kv_heads
    query_heads = queries.reshape(slot_count, kv_heads, groups, head_dim)
    key_part = kv_block[..., :head_dim]
    value_part = kv_block[..., head_dim:]
    score_scale = head_dim ** (-0.5)
    scores = (
        jnp.einsum("skgd,sckd->skgc", query_heads, key_part, preferred_element_type=F32)
        * score_scale
    )
    live_mask = (jnp.arange(context, dtype=jnp.int32)[None, :] < lengths[:, None])[:, None, None, :]
    scores = jnp.where(live_mask, scores, -1e30)
    own_score = (
        jnp.einsum(
            "skgd,skd->skg", query_heads, fresh_kv[..., :head_dim], preferred_element_type=F32
        )
        * score_scale
    )
    highest = jnp.maximum(jnp.max(scores, axis=-1), own_score)
    weights = jnp.where(live_mask, jnp.exp(scores - highest[..., None]), 0.0)
    own_weight = jnp.exp(own_score - highest)
    total_weight = jnp.sum(weights, axis=-1) + own_weight
    own_round = lax.reduce_precision(own_weight, 8, 7)
    mixed_sum = jnp.einsum(
        "skgc,sckd->skgd", weights.astype(BF), value_part, preferred_element_type=F32
    )
    mixed_sum = mixed_sum + own_round[..., None] * fresh_kv[:, :, None, head_dim:].astype(F32)
    return (mixed_sum / total_weight[..., None]).reshape(slot_count, -1).astype(BF)


def share(values, axes, count):
    stacked = jnp.broadcast_to(values[None], (count,) + values.shape)
    return lax.all_to_all(stacked, axes, 0, 0, tiled=True)


def on_device(
    queries,
    new_kv,
    residual,
    kv_cache,
    cache_len,
    request_perm,
    expert_ids,
    route_wt,
    attn_out_w,
    post_gain,
    expert_gate_up,
    expert_down,
    final_gain,
    vocab_w,
):
    ix, iz, ic, iy = (lax.axis_index(a) for a in ALL)
    rows = queries.shape[0]
    groups = X * Z * C
    total = groups * rows
    group_index = (ix * Z + iz) * C + ic
    col = residual.shape[1]
    width = attn_out_w.shape[1]
    kv_width = new_kv.shape[2]
    head_dim = kv_width // 2
    top_count = expert_ids.shape[1]
    cap = 2
    int_range = lambda n: jnp.arange(n, dtype=jnp.int32)

    packed = jnp.concatenate([queries, new_kv.reshape(rows, kv_width), residual], axis=1)
    plane = share(packed, ("x", "c"), X * C).reshape(X * C * rows, -1)
    plane_slots = lax.dynamic_index_in_dim(
        request_perm.reshape(X, Z, C * rows), iz, 1, keepdims=False
    ).reshape(-1)
    wanted_slots = (((ix * Z + int_range(Z)) * C + ic) * rows)[:, None] + int_range(rows)[None, :]
    select = (wanted_slots.reshape(-1)[:, None] == plane_slots[None, :]).astype(BF)
    outgoing = jnp.dot(select, plane, preferred_element_type=F32).astype(BF)
    arrived = lax.all_to_all(outgoing.reshape(Z, rows, -1), "z", 0, 0, tiled=True)
    mine = jnp.sum(arrived.astype(F32), axis=0).astype(BF)
    mine_q = mine[:, :col]
    mine_kv = mine[:, col : col + kv_width].reshape(rows, 1, kv_width)
    mine_res = mine[:, col + kv_width :]

    attended = attend(mine_q, mine_kv, kv_cache, cache_len, head_dim)
    partial_value = jnp.dot(attended, attn_out_w, preferred_element_type=F32).astype(BF)
    parts = share(jnp.concatenate([partial_value, mine_res], axis=1), "y", Y)
    full_res = jnp.concatenate([parts[t, :, width:] for t in range(Y)], axis=1).astype(F32)
    mixed_full = full_res + jnp.sum(parts[:, :, :width].astype(F32), axis=0)
    mixed_cols = lax.dynamic_slice_in_dim(mixed_full, iy * col, col, 1)
    scale_rows = lax.rsqrt(jnp.mean(mixed_full * mixed_full, axis=1, keepdims=True) + epsilon)
    normed = (mixed_full * scale_rows * post_gain).astype(BF)

    hits = expert_ids[:, :, None] == int_range(groups)[None, None, :]
    row_hits = jnp.sum(hits.astype(jnp.int32), axis=1)
    rank = jnp.cumsum(row_hits, axis=0) - row_hits
    place = (row_hits[:, :, None] > 0) & (rank[:, :, None] == int_range(cap)[None, None, :])
    place = place.reshape(rows, groups * cap)
    route_share = route_wt / jnp.sum(route_wt, axis=1, keepdims=True)
    row_share = jnp.sum(jnp.where(hits, route_share[:, :, None], 0.0), axis=1)
    blend = jnp.where(
        place,
        jnp.broadcast_to(row_share[:, :, None], (rows, groups, cap)).reshape(rows, -1),
        0.0,
    )
    sent = jnp.dot(place.T.astype(BF), normed, preferred_element_type=F32).astype(BF)
    inbound = lax.all_to_all(sent.reshape(groups, cap, width), REQ, 0, 0, tiled=True)
    inbound = inbound.reshape(groups * cap, width)
    gate_val = jnp.dot(inbound, expert_gate_up[0, 0], preferred_element_type=F32)
    upward = jnp.dot(inbound, expert_gate_up[0, 1], preferred_element_type=F32)
    active = (jax.nn.silu(gate_val) * upward).astype(BF)
    produced = jnp.dot(active, expert_down[0], preferred_element_type=F32).astype(BF)

    produced = produced.reshape(groups, cap, Y, col).transpose(0, 2, 1, 3)
    returned = lax.all_to_all(
        produced.reshape(groups * Y, cap, col), ALL, 0, 0, tiled=True
    ).reshape(groups * Y * cap, col)
    blend = jnp.broadcast_to(
        blend.reshape(rows, groups, 1, cap), (rows, groups, Y, cap)
    ).reshape(rows, -1)
    blend_high = lax.reduce_precision(blend, 8, 7)
    blend_two = jnp.concatenate([blend_high, blend - blend_high], axis=0).astype(BF)
    moe_two = jnp.dot(blend_two, returned, preferred_element_type=F32)
    state_cols = (mixed_cols + moe_two[:rows] + moe_two[rows:]).astype(BF)

    by_zy = share(state_cols, ("z", "y"), Z * Y)
    by_x = share(by_zy, ("x",), X)
    other = lax.ppermute(by_x, "c", [(0, 1), (1, 0)])
    first = jnp.where(ic == 0, by_x, other)
    second = jnp.where(ic == 0, other, by_x)
    every = jnp.stack([first, second]).reshape(C, X, Z, Y, rows, col)
    chunks = [every[:, :, :, t].reshape(total, col) for t in range(Y)]
    slot_of = (
        ((int_range(X)[None, :, None] * Z + int_range(Z)[None, None, :]) * C)
        + int_range(C)[:, None, None]
    )[..., None] * rows + int_range(rows)
    slot_of = slot_of.reshape(-1)
    square = sum(jnp.sum(jnp.square(c.astype(F32)), axis=1) for c in chunks)
    mean_eps = square / width + epsilon
    row_scale = lax.rsqrt(mean_eps)[:, None]
    logits = 0.0
    for t, c in enumerate(chunks):
        ready = (c.astype(F32) * row_scale * final_gain[t * col : (t + 1) * col]).astype(BF)
        logits = logits + lax.dot_general(
            ready,
            vocab_w[:, t * col : (t + 1) * col],
            (((1,), (1,)), ((), ())),
            preferred_element_type=F32,
        )
    local_top = jnp.max(logits, axis=1)
    pick = request_perm[:, None] == slot_of[None, :]
    top_by_request = jnp.sum(jnp.where(pick, local_top[None, :], 0.0), axis=1)
    tops = jnp.broadcast_to(top_by_request.reshape(groups, 1, rows), (groups, Y, rows))
    tops = lax.all_to_all(tops.reshape(groups * Y, rows), ALL, 0, 0, tiled=True)
    top_logit = jnp.max(tops, axis=0)

    wanted = lax.dynamic_slice_in_dim(request_perm, group_index * rows, rows)
    back = wanted[:, None] == slot_of[None, :]
    own_chunk = lax.dynamic_index_in_dim(every, iy, 3, keepdims=False).reshape(total, col)
    hidden_out = jnp.dot(back.astype(BF), own_chunk, preferred_element_type=F32).astype(BF)
    state_norm = jnp.sqrt(jnp.sum(jnp.where(back, mean_eps[None, :], 0.0), axis=1))
    return (hidden_out, state_norm, top_logit)


def solution(mesh):
    fine = Mesh(mesh.devices.reshape(X, Z, C, Y), ALL)
    placed = (
        P(REQ, "y"),
        P(REQ, "y", None),
        P(REQ, "y"),
        P(REQ, None, "y", None),
        P(REQ),
        P(),
        P(REQ, None),
        P(REQ, None),
        P("y", None),
        P(),
        P(REQ, None, None, "y"),
        P(REQ, "y", None),
        P(),
        P(ALL, None),
    )
    return jax.shard_map(
        on_device,
        mesh=fine,
        in_specs=placed,
        out_specs=(P(REQ, "y"), P(REQ), P(REQ)),
        check_vma=False,
    )
```

```python
import jax
import jax.numpy as jnp
from jax import lax
from jax.sharding import Mesh, PartitionSpec as P

epsilon = 1e-05
X, Z, C, Y = 4, 8, 2, 4
REQ = ("x", "z", "c")
ALL = ("x", "z", "c", "y")
BF = jnp.bfloat16
F32 = jnp.float32


def attend(queries, fresh_kv, kv_block, lengths, head_dim):
    slot_count, context, kv_heads, _ = kv_block.shape
    groups = queries.shape[1] // head_dim // kv_heads
    query_heads = queries.reshape(slot_count, kv_heads, groups, head_dim)
    key_part = kv_block[..., :head_dim]
    value_part = kv_block[..., head_dim:]
    score_scale = head_dim ** (-0.5)
    scores = (
        jnp.einsum("skgd,sckd->skgc", query_heads, key_part, preferred_element_type=F32)
        * score_scale
    )
    live_mask = (jnp.arange(context, dtype=jnp.int32)[None, :] < lengths[:, None])[:, None, None, :]
    scores = jnp.where(live_mask, scores, -1e30)
    own_score = (
        jnp.einsum(
            "skgd,skd->skg", query_heads, fresh_kv[..., :head_dim], preferred_element_type=F32
        )
        * score_scale
    )
    highest = jnp.maximum(jnp.max(scores, axis=-1), own_score)
    weights = jnp.where(live_mask, jnp.exp(scores - highest[..., None]), 0.0)
    own_weight = jnp.exp(own_score - highest)
    total_weight = jnp.sum(weights, axis=-1) + own_weight
    own_round = lax.reduce_precision(own_weight, 8, 7)
    mixed_sum = jnp.einsum(
        "skgc,sckd->skgd", weights.astype(BF), value_part, preferred_element_type=F32
    )
    mixed_sum = mixed_sum + own_round[..., None] * fresh_kv[:, :, None, head_dim:].astype(F32)
    return (mixed_sum / total_weight[..., None]).reshape(slot_count, -1).astype(BF)


def share(values, axes, count):
    stacked = jnp.broadcast_to(values[None], (count,) + values.shape)
    return lax.all_to_all(stacked, axes, 0, 0, tiled=True)


def on_device(
    queries,
    new_kv,
    residual,
    kv_cache,
    cache_len,
    request_perm,
    expert_ids,
    route_wt,
    attn_out_w,
    post_gain,
    expert_gate_up,
    expert_down,
    final_gain,
    vocab_w,
):
    vocab_other = lax.ppermute(vocab_w, "c", [(0, 1), (1, 0)])
    ix, iz, ic, iy = (lax.axis_index(a) for a in ALL)
    rows = queries.shape[0]
    groups = X * Z * C
    col = residual.shape[1]
    width = attn_out_w.shape[1]
    kv_width = new_kv.shape[2]
    head_dim = kv_width // 2
    top_count = expert_ids.shape[1]
    cap = 2
    int_range = lambda n: jnp.arange(n, dtype=jnp.int32)

    packed = jnp.concatenate([queries, new_kv.reshape(rows, kv_width), residual], axis=1)
    plane = share(packed, ("x", "c"), X * C).reshape(X * C * rows, -1)
    plane_slots = lax.dynamic_index_in_dim(
        request_perm.reshape(X, Z, C * rows), iz, 1, keepdims=False
    ).reshape(-1)
    wanted_slots = (((ix * Z + int_range(Z)) * C + ic) * rows)[:, None] + int_range(rows)[None, :]
    select = (wanted_slots.reshape(-1)[:, None] == plane_slots[None, :]).astype(BF)
    outgoing = jnp.dot(select, plane, preferred_element_type=F32).astype(BF)
    arrived = lax.all_to_all(outgoing.reshape(Z, rows, -1), "z", 0, 0, tiled=True)
    mine = jnp.sum(arrived.astype(F32), axis=0).astype(BF)
    mine_q = mine[:, :col]
    mine_kv = mine[:, col : col + kv_width].reshape(rows, 1, kv_width)
    mine_res = mine[:, col + kv_width :]

    attended = attend(mine_q, mine_kv, kv_cache, cache_len, head_dim)
    partial_value = jnp.dot(attended, attn_out_w, preferred_element_type=F32).astype(BF)
    parts = share(jnp.concatenate([partial_value, mine_res], axis=1), "y", Y)
    full_res = jnp.concatenate([parts[t, :, width:] for t in range(Y)], axis=1).astype(F32)
    mixed_full = full_res + jnp.sum(parts[:, :, :width].astype(F32), axis=0)
    mixed_cols = lax.dynamic_slice_in_dim(mixed_full, iy * col, col, 1)
    scale_rows = lax.rsqrt(jnp.mean(mixed_full * mixed_full, axis=1, keepdims=True) + epsilon)
    normed = (mixed_full * scale_rows * post_gain).astype(BF)

    hits = expert_ids[:, :, None] == int_range(groups)[None, None, :]
    row_hits = jnp.sum(hits.astype(jnp.int32), axis=1)
    rank = jnp.cumsum(row_hits, axis=0) - row_hits
    place = (row_hits[:, :, None] > 0) & (rank[:, :, None] == int_range(cap)[None, None, :])
    place = place.reshape(rows, groups * cap)
    route_share = route_wt / jnp.sum(route_wt, axis=1, keepdims=True)
    row_share = jnp.sum(jnp.where(hits, route_share[:, :, None], 0.0), axis=1)
    blend = jnp.where(
        place,
        jnp.broadcast_to(row_share[:, :, None], (rows, groups, cap)).reshape(rows, -1),
        0.0,
    )
    pairs = groups * cap
    lines = pairs * Y
    spread = jnp.repeat(place.astype(BF), Y, axis=1)
    chunk_of_line = (int_range(lines) % Y)[None, :]
    spread = jnp.concatenate(
        [jnp.where(chunk_of_line == t, spread, 0) for t in range(Y)], axis=0
    )
    tall = jnp.concatenate([normed[:, t * col : (t + 1) * col] for t in range(Y)], axis=0)
    sent = lax.dot_general(
        spread, tall, (((0,), (0,)), ((), ())), preferred_element_type=F32
    ).astype(BF)
    inbound = lax.all_to_all(sent.reshape(groups, cap * Y, col), REQ, 0, 0, tiled=True)
    by_chunk = int_range(lines)
    by_chunk = by_chunk % pairs * Y + by_chunk // pairs
    order = (by_chunk[:, None] == int_range(lines)[None, :]).astype(BF)
    inbound = jnp.dot(order, inbound.reshape(lines, col), preferred_element_type=F32).astype(BF)
    inbound = jnp.concatenate([inbound[t * pairs : (t + 1) * pairs] for t in range(Y)], axis=1)
    gate_val = jnp.dot(inbound, expert_gate_up[0, 0], preferred_element_type=F32)
    upward = jnp.dot(inbound, expert_gate_up[0, 1], preferred_element_type=F32)
    active = (jax.nn.silu(gate_val) * upward).astype(BF)
    produced = jnp.dot(active, expert_down[0], preferred_element_type=F32).astype(BF)

    produced = jnp.concatenate([produced[:, t * col : (t + 1) * col] for t in range(Y)], axis=0)
    produced = lax.dot_general(
        order, produced, (((0,), (0,)), ((), ())), preferred_element_type=F32
    ).astype(BF)
    returned = lax.all_to_all(
        produced.reshape(groups, cap * Y, col), REQ, 0, 0, tiled=True
    ).reshape(lines, col)
    blend = jnp.repeat(blend, Y, axis=1)
    blend = jnp.concatenate(
        [jnp.where(chunk_of_line == t, blend, 0.0) for t in range(Y)], axis=0
    )
    blend_high = lax.reduce_precision(blend, 8, 7)
    blend_two = jnp.concatenate([blend_high, blend - blend_high], axis=0).astype(BF)
    moe_two = jnp.dot(blend_two, returned, preferred_element_type=F32)
    moe_part = (moe_two[: Y * rows] + moe_two[Y * rows :]).astype(BF).reshape(Y, rows, col)
    moe_cols = lax.all_to_all(moe_part, "y", 0, 0, tiled=True)
    state_cols = (mixed_cols + jnp.sum(moe_cols.astype(F32), axis=0)).astype(BF)

    by_zy = share(state_cols, ("z", "y"), Z * Y)
    by_x = share(by_zy, ("x",), X).reshape(X, Z, Y, rows, col)
    every = by_x.transpose(2, 0, 1, 3, 4)
    chunks = [by_x[:, :, t].reshape(X * Z * rows, col) for t in range(Y)]
    half = X * Z * rows
    slot_of = ((int_range(X)[:, None] * Z + int_range(Z)[None, :]) * C + ic)[..., None]
    slot_of = (slot_of * rows + int_range(rows)).reshape(-1)
    square = sum(jnp.sum(jnp.square(c.astype(F32)), axis=1) for c in chunks)
    mean_eps = square / width + epsilon
    logits = 0.0
    logits_other = 0.0
    for t, c in enumerate(chunks):
        gained = (c.astype(F32) * final_gain[t * col : (t + 1) * col]).astype(BF)
        cut = slice(t * col, (t + 1) * col)
        meet = (((1,), (1,)), ((), ()))
        logits = logits + lax.dot_general(
            gained, vocab_w[:, cut], meet, preferred_element_type=F32
        )
        logits_other = logits_other + lax.dot_general(
            gained, vocab_other[:, cut], meet, preferred_element_type=F32
        )
    local_top = jnp.maximum(jnp.max(logits, axis=1), jnp.max(logits_other, axis=1))
    local_top = local_top * lax.rsqrt(mean_eps)
    pick = request_perm[:, None] == slot_of[None, :]
    top_by_request = jnp.max(jnp.where(pick, local_top[None, :], -jnp.inf), axis=1)
    tops = jnp.broadcast_to(top_by_request.reshape(groups, 1, rows), (groups, Y, rows))
    tops = lax.all_to_all(tops.reshape(groups * Y, rows), ALL, 0, 0, tiled=True)
    top_logit = jnp.max(tops, axis=0)

    chip_rows = C * rows
    wanted = lax.dynamic_slice_in_dim(request_perm, (ix * Z + iz) * chip_rows, chip_rows)
    back = wanted[:, None] == slot_of[None, :]
    own_chunk = lax.dynamic_index_in_dim(every, iy, 0, keepdims=False).reshape(half, col)
    found = jnp.dot(back.astype(BF), own_chunk, preferred_element_type=F32).astype(BF)
    found_mean = jnp.sum(jnp.where(back, mean_eps[None, :], 0.0), axis=1)
    found = found.reshape(C, rows, col)
    found_mean = found_mean.reshape(C, rows)
    swap = [(0, 1), (1, 0)]
    crossed = lax.ppermute(jnp.where(ic == 0, found[1], found[0]), "c", swap)
    crossed_mean = lax.ppermute(jnp.where(ic == 0, found_mean[1], found_mean[0]), "c", swap)
    kept = jnp.where(ic == 0, found[0], found[1])
    kept_mean = jnp.where(ic == 0, found_mean[0], found_mean[1])
    hidden_out = (kept.astype(F32) + crossed.astype(F32)).astype(BF)
    state_norm = jnp.sqrt(kept_mean + crossed_mean)
    return (hidden_out, state_norm, top_logit)


def solution(mesh):
    fine = Mesh(mesh.devices.reshape(X, Z, C, Y), ALL)
    placed = (
        P(REQ, "y"),
        P(REQ, "y", None),
        P(REQ, "y"),
        P(REQ, None, "y", None),
        P(REQ),
        P(),
        P(REQ, None),
        P(REQ, None),
        P("y", None),
        P(),
        P(REQ, None, None, "y"),
        P(REQ, "y", None),
        P(),
        P(ALL, None),
    )
    return jax.shard_map(
        on_device,
        mesh=fine,
        in_specs=placed,
        out_specs=(P(REQ, "y"), P(REQ), P(REQ)),
        check_vma=False,
    )
```

```python
import jax
import jax.numpy as jnp
from jax import lax
from jax.experimental import pallas as pl
from jax.experimental.pallas import tpu as pltpu
from jax.sharding import Mesh, PartitionSpec as P

epsilon = 1e-05
X, Z, C, Y = 4, 8, 2, 4
REQ = ("x", "z", "c")
ALL = ("x", "z", "c", "y")
BF = jnp.bfloat16
F32 = jnp.float32


def attend(queries, fresh_kv, kv_block, lengths, head_dim):
    slot_count, context, kv_heads, _ = kv_block.shape
    groups = queries.shape[1] // head_dim // kv_heads
    query_heads = queries.reshape(slot_count, kv_heads, groups, head_dim)
    key_part = kv_block[..., :head_dim]
    value_part = kv_block[..., head_dim:]
    score_scale = head_dim ** (-0.5)
    scores = (
        jnp.einsum("skgd,sckd->skgc", query_heads, key_part, preferred_element_type=F32)
        * score_scale
    )
    live_mask = (jnp.arange(context, dtype=jnp.int32)[None, :] < lengths[:, None])[:, None, None, :]
    scores = jnp.where(live_mask, scores, -1e30)
    own_score = (
        jnp.einsum(
            "skgd,skd->skg", query_heads, fresh_kv[..., :head_dim], preferred_element_type=F32
        )
        * score_scale
    )
    highest = jnp.maximum(jnp.max(scores, axis=-1), own_score)
    weights = jnp.where(live_mask, jnp.exp(scores - highest[..., None]), 0.0)
    own_weight = jnp.exp(own_score - highest)
    total_weight = jnp.sum(weights, axis=-1) + own_weight
    own_round = lax.reduce_precision(own_weight, 8, 7)
    mixed_sum = jnp.einsum(
        "skgc,sckd->skgd", weights.astype(BF), value_part, preferred_element_type=F32
    )
    mixed_sum = mixed_sum + own_round[..., None] * fresh_kv[:, :, None, head_dim:].astype(F32)
    return (mixed_sum / total_weight[..., None]).reshape(slot_count, -1).astype(BF)


def share(values, axes, count):
    stacked = jnp.broadcast_to(values[None], (count,) + values.shape)
    return lax.all_to_all(stacked, axes, 0, 0, tiled=True)


def route_kernel(groups, cap, ids_ref, wt_ref, spread_ref, blend_ref):
    rows, top_count = ids_ref.shape
    lines = groups * cap * Y
    line = lax.broadcasted_iota(jnp.int32, (rows, lines), 1)
    expert = line // (cap * Y)
    slot = (line // Y) % cap
    chunk = line % Y
    ids = ids_ref[...]
    weights = wt_ref[...]
    share_of = weights / jnp.sum(weights, axis=1, keepdims=True)
    hit = jnp.zeros((rows, lines), F32)
    share_row = jnp.zeros((rows, lines), F32)
    for j in range(top_count):
        same = ids[:, j : j + 1] == expert
        hit = jnp.where(same, 1.0, hit)
        share_row = jnp.where(same, share_of[:, j : j + 1], share_row)
    earlier = jnp.zeros((1, lines), F32)
    ranks = []
    for r in range(rows):
        ranks.append(earlier)
        earlier = earlier + hit[r : r + 1]
    rank = jnp.concatenate(ranks, axis=0)
    placed = jnp.where(rank == slot.astype(F32), hit, 0.0)
    blend = placed * share_row
    high = blend.astype(BF).astype(F32)
    low = blend - high
    for t in range(Y):
        here = chunk == t
        lo, hi = t * rows, (t + 1) * rows
        spread_ref[lo:hi, :] = jnp.where(here, placed, 0.0)
        blend_ref[lo:hi, :] = jnp.where(here, high, 0.0)
        blend_ref[Y * rows + lo : Y * rows + hi, :] = jnp.where(here, low, 0.0)


def route_tables(expert_ids, route_wt, groups, cap):
    rows = expert_ids.shape[0]
    lines = groups * cap * Y
    return pl.pallas_call(
        lambda *refs: route_kernel(groups, cap, *refs),
        out_shape=(
            jax.ShapeDtypeStruct((Y * rows, lines), F32),
            jax.ShapeDtypeStruct((2 * Y * rows, lines), F32),
        ),
        name="route_tables",
    )(expert_ids, route_wt)


def expert_kernel(in_ref, up_ref, down_ref, out_ref, x_ref, acc_ref):
    step = pl.program_id(0)
    lines, col = in_ref.shape
    pairs = lines // Y

    @pl.when(step == 0)
    def _():
        target = lax.broadcasted_iota(jnp.int32, (lines, lines), 0)
        origin = lax.broadcasted_iota(jnp.int32, (lines, lines), 1)
        order = jnp.where(target % pairs * Y + target // pairs == origin, 1.0, 0.0).astype(BF)
        sorted_rows = jnp.dot(order, in_ref[...], preferred_element_type=F32).astype(BF)
        for t in range(Y):
            x_ref[:, t * col : (t + 1) * col] = sorted_rows[t * pairs : (t + 1) * pairs]
        acc_ref[...] = jnp.zeros_like(acc_ref)

    x = x_ref[...]
    gate_val = jnp.dot(x, up_ref[0, 0], preferred_element_type=F32)
    upward = jnp.dot(x, up_ref[0, 1], preferred_element_type=F32)
    active = (gate_val / (1.0 + jnp.exp(-gate_val)) * upward).astype(BF)
    acc_ref[...] += jnp.dot(active, down_ref[0], preferred_element_type=F32)

    @pl.when(step == pl.num_programs(0) - 1)
    def _():
        target = lax.broadcasted_iota(jnp.int32, (lines, lines), 0)
        origin = lax.broadcasted_iota(jnp.int32, (lines, lines), 1)
        order = jnp.where(origin % pairs * Y + origin // pairs == target, 1.0, 0.0).astype(BF)
        for t in range(Y):
            x_ref[:, t * col : (t + 1) * col] = acc_ref[:, t * col : (t + 1) * col].astype(BF)
        tall = jnp.concatenate([x_ref[:, t * col : (t + 1) * col] for t in range(Y)], axis=0)
        out_ref[...] = jnp.dot(order, tall, preferred_element_type=F32).astype(BF)


def run_expert(inbound, gate_up, down):
    lines, col = inbound.shape
    _, _, width, hidden = gate_up.shape
    block = 128
    return pl.pallas_call(
        expert_kernel,
        grid=(hidden // block,),
        in_specs=[
            pl.BlockSpec((lines, col), lambda i: (0, 0)),
            pl.BlockSpec((1, 2, width, block), lambda i: (0, 0, 0, i)),
            pl.BlockSpec((1, block, width), lambda i: (0, i, 0)),
        ],
        out_specs=pl.BlockSpec((lines, col), lambda i: (0, 0)),
        out_shape=jax.ShapeDtypeStruct((lines, col), BF),
        scratch_shapes=[
            pltpu.VMEM((lines // Y, width), BF),
            pltpu.VMEM((lines // Y, width), F32),
        ],
        name="run_expert",
    )(inbound, gate_up, down)


def on_device(
    queries,
    new_kv,
    residual,
    kv_cache,
    cache_len,
    request_perm,
    expert_ids,
    route_wt,
    attn_out_w,
    post_gain,
    expert_gate_up,
    expert_down,
    final_gain,
    vocab_w,
):
    vocab_other = lax.ppermute(vocab_w, "c", [(0, 1), (1, 0)])
    ix, iz, ic, iy = (lax.axis_index(a) for a in ALL)
    rows = queries.shape[0]
    groups = X * Z * C
    col = residual.shape[1]
    width = attn_out_w.shape[1]
    kv_width = new_kv.shape[2]
    head_dim = kv_width // 2
    cap = 2
    int_range = lambda n: jnp.arange(n, dtype=jnp.int32)

    packed = jnp.concatenate([queries, new_kv.reshape(rows, kv_width), residual], axis=1)
    plane = share(packed, ("x", "c"), X * C).reshape(X * C * rows, -1)
    plane_slots = lax.dynamic_index_in_dim(
        request_perm.reshape(X, Z, C * rows), iz, 1, keepdims=False
    ).reshape(-1)
    wanted_slots = (((ix * Z + int_range(Z)) * C + ic) * rows)[:, None] + int_range(rows)[None, :]
    select = (wanted_slots.reshape(-1)[:, None] == plane_slots[None, :]).astype(BF)
    outgoing = jnp.dot(select, plane, preferred_element_type=F32).astype(BF)
    arrived = lax.all_to_all(outgoing.reshape(Z, rows, -1), "z", 0, 0, tiled=True)
    mine = jnp.sum(arrived.astype(F32), axis=0).astype(BF)
    mine_q = mine[:, :col]
    mine_kv = mine[:, col : col + kv_width].reshape(rows, 1, kv_width)
    mine_res = mine[:, col + kv_width :]

    attended = attend(mine_q, mine_kv, kv_cache, cache_len, head_dim)
    partial_value = jnp.dot(attended, attn_out_w, preferred_element_type=F32).astype(BF)
    parts = share(jnp.concatenate([partial_value, mine_res], axis=1), "y", Y)
    full_res = jnp.concatenate([parts[t, :, width:] for t in range(Y)], axis=1).astype(F32)
    mixed_full = full_res + jnp.sum(parts[:, :, :width].astype(F32), axis=0)
    scale_rows = lax.rsqrt(jnp.mean(mixed_full * mixed_full, axis=1, keepdims=True) + epsilon)
    normed = (mixed_full * scale_rows * post_gain).astype(BF)

    spread, blend_two = route_tables(expert_ids, route_wt, groups, cap)
    lines = groups * cap * Y
    tall = jnp.concatenate([normed[:, t * col : (t + 1) * col] for t in range(Y)], axis=0)
    sent = lax.dot_general(
        spread.astype(BF), tall, (((0,), (0,)), ((), ())), preferred_element_type=F32
    ).astype(BF)
    inbound = lax.all_to_all(sent.reshape(groups, cap * Y, col), REQ, 0, 0, tiled=True)
    produced = run_expert(inbound.reshape(lines, col), expert_gate_up, expert_down)

    returned = lax.all_to_all(
        produced.reshape(groups, cap * Y, col), REQ, 0, 0, tiled=True
    ).reshape(lines, col)
    moe_two = jnp.dot(blend_two.astype(BF), returned, preferred_element_type=F32)
    moe_part = (moe_two[: Y * rows] + moe_two[Y * rows :]).astype(BF)
    moe_part = jnp.concatenate([moe_part[t * rows : (t + 1) * rows] for t in range(Y)], axis=1)
    moe_full = jnp.sum(share(moe_part, "y", Y).astype(F32), axis=0)
    state = (mixed_full + moe_full).astype(BF)

    half = X * Z * rows
    every = share(share(state, ("z",), Z), ("x",), X).reshape(half, width)
    slot_of = ((int_range(X)[:, None] * Z + int_range(Z)[None, :]) * C + ic)[..., None]
    slot_of = (slot_of * rows + int_range(rows)).reshape(-1)
    gained = (every.astype(F32) * final_gain).astype(BF)
    meet = (((1,), (1,)), ((), ()))
    logits = lax.dot_general(gained, vocab_w, meet, preferred_element_type=F32)
    logits_other = lax.dot_general(gained, vocab_other, meet, preferred_element_type=F32)
    local_top = jnp.maximum(jnp.max(logits, axis=1), jnp.max(logits_other, axis=1))
    pick = request_perm[:, None] == slot_of[None, :]
    top_by_request = jnp.max(jnp.where(pick, local_top[None, :], -jnp.inf), axis=1)
    every, top_by_request = lax.optimization_barrier((every, top_by_request))
    tops = jnp.broadcast_to(top_by_request.reshape(groups, 1, rows), (groups, Y, rows))
    tops = lax.all_to_all(tops.reshape(groups * Y, rows), ALL, 0, 0, tiled=True)

    chip_rows = C * rows
    wanted = lax.dynamic_slice_in_dim(request_perm, (ix * Z + iz) * chip_rows, chip_rows)
    back = wanted[:, None] == slot_of[None, :]
    found = jnp.dot(back.astype(BF), every, preferred_element_type=F32).astype(BF)
    crossed = lax.ppermute(
        jnp.where(ic == 0, found[rows:], found[:rows]), "c", [(0, 1), (1, 0)]
    )
    hidden = jnp.where(ic == 0, found[:rows], found[rows:]).astype(F32) + crossed.astype(F32)
    hidden_out = lax.dynamic_slice_in_dim(hidden, iy * col, col, 1).astype(BF)
    mean_eps = jnp.mean(hidden * hidden, axis=1) + epsilon
    top_logit = jnp.max(tops, axis=0) * lax.rsqrt(mean_eps)
    return (hidden_out, jnp.sqrt(mean_eps), top_logit)


def solution(mesh):
    fine = Mesh(mesh.devices.reshape(X, Z, C, Y), ALL)
    placed = (
        P(REQ, "y"),
        P(REQ, "y", None),
        P(REQ, "y"),
        P(REQ, None, "y", None),
        P(REQ),
        P(),
        P(REQ, None),
        P(REQ, None),
        P("y", None),
        P(),
        P(REQ, None, None, "y"),
        P(REQ, "y", None),
        P(),
        P(ALL, None),
    )
    return jax.shard_map(
        on_device,
        mesh=fine,
        in_specs=placed,
        out_specs=(P(REQ, "y"), P(REQ), P(REQ)),
        check_vma=False,
    )
```

```python
import jax
import jax.numpy as jnp
from jax import lax
from jax.experimental import pallas as pl
from jax.experimental.pallas import tpu as pltpu
from jax.sharding import Mesh, PartitionSpec as P

epsilon = 1e-05
X, Z, C, Y = 4, 8, 2, 4
REQ = ("x", "z", "c")
ALL = ("x", "z", "c", "y")
BF = jnp.bfloat16
F32 = jnp.float32


def attend(queries, fresh_kv, kv_block, lengths, head_dim):
    slot_count, context, kv_heads, _ = kv_block.shape
    groups = queries.shape[1] // head_dim // kv_heads
    query_heads = queries.reshape(slot_count, kv_heads, groups, head_dim)
    key_part = kv_block[..., :head_dim]
    value_part = kv_block[..., head_dim:]
    score_scale = head_dim ** (-0.5)
    scores = (
        jnp.einsum("skgd,sckd->skgc", query_heads, key_part, preferred_element_type=F32)
        * score_scale
    )
    live_mask = (jnp.arange(context, dtype=jnp.int32)[None, :] < lengths[:, None])[:, None, None, :]
    scores = jnp.where(live_mask, scores, -1e30)
    own_score = (
        jnp.einsum(
            "skgd,skd->skg", query_heads, fresh_kv[..., :head_dim], preferred_element_type=F32
        )
        * score_scale
    )
    highest = jnp.maximum(jnp.max(scores, axis=-1), own_score)
    weights = jnp.where(live_mask, jnp.exp(scores - highest[..., None]), 0.0)
    own_weight = jnp.exp(own_score - highest)
    total_weight = jnp.sum(weights, axis=-1) + own_weight
    own_round = lax.reduce_precision(own_weight, 8, 7)
    mixed_sum = jnp.einsum(
        "skgc,sckd->skgd", weights.astype(BF), value_part, preferred_element_type=F32
    )
    mixed_sum = mixed_sum + own_round[..., None] * fresh_kv[:, :, None, head_dim:].astype(F32)
    return (mixed_sum / total_weight[..., None]).reshape(slot_count, -1).astype(BF)


def share(values, axes, count):
    stacked = jnp.broadcast_to(values[None], (count,) + values.shape)
    return lax.all_to_all(stacked, axes, 0, 0, tiled=True)


def route_kernel(groups, cap, ids_ref, wt_ref, spread_ref, blend_ref):
    rows, top_count = ids_ref.shape
    lines = groups * cap * Y
    line = lax.broadcasted_iota(jnp.int32, (rows, lines), 1)
    expert = line // (cap * Y)
    slot = (line // Y) % cap
    chunk = line % Y
    ids = ids_ref[...]
    weights = wt_ref[...]
    share_of = weights / jnp.sum(weights, axis=1, keepdims=True)
    hit = jnp.zeros((rows, lines), F32)
    share_row = jnp.zeros((rows, lines), F32)
    for j in range(top_count):
        same = ids[:, j : j + 1] == expert
        hit = jnp.where(same, 1.0, hit)
        share_row = jnp.where(same, share_of[:, j : j + 1], share_row)
    earlier = jnp.zeros((1, lines), F32)
    ranks = []
    for r in range(rows):
        ranks.append(earlier)
        earlier = earlier + hit[r : r + 1]
    rank = jnp.concatenate(ranks, axis=0)
    placed = jnp.where(rank == slot.astype(F32), hit, 0.0)
    blend = placed * share_row
    high = blend.astype(BF).astype(F32)
    low = blend - high
    for t in range(Y):
        here = chunk == t
        lo, hi = t * rows, (t + 1) * rows
        spread_ref[lo:hi, :] = jnp.where(here, placed, 0.0)
        blend_ref[lo:hi, :] = jnp.where(here, high, 0.0)
        blend_ref[Y * rows + lo : Y * rows + hi, :] = jnp.where(here, low, 0.0)


def route_tables(expert_ids, route_wt, groups, cap):
    rows = expert_ids.shape[0]
    lines = groups * cap * Y
    return pl.pallas_call(
        lambda *refs: route_kernel(groups, cap, *refs),
        out_shape=(
            jax.ShapeDtypeStruct((Y * rows, lines), F32),
            jax.ShapeDtypeStruct((2 * Y * rows, lines), F32),
        ),
        name="route_tables",
    )(expert_ids, route_wt)


def mix_kernel(parts_ref, gain_ref, spread_ref, mixed_ref, sent_ref):
    width = gain_ref.shape[1]
    col = width // Y
    total = parts_ref[0, :, :width].astype(F32)
    for t in range(1, Y):
        total = total + parts_ref[t, :, :width].astype(F32)
    pieces = [
        total[:, t * col : (t + 1) * col] + parts_ref[t, :, width:].astype(F32)
        for t in range(Y)
    ]
    square = sum(jnp.sum(p * p, axis=1, keepdims=True) for p in pieces)
    scale = lax.rsqrt(square / width + epsilon)
    tall = []
    for t, p in enumerate(pieces):
        mixed_ref[:, t * col : (t + 1) * col] = p
        tall.append(p * scale * gain_ref[:, t * col : (t + 1) * col])
    tall = jnp.concatenate(tall, axis=0).astype(BF)
    sent_ref[...] = lax.dot_general(
        spread_ref[...].astype(BF), tall, (((0,), (0,)), ((), ())), preferred_element_type=F32
    ).astype(BF)


def mix_rows(parts, gain, spread):
    rows = parts.shape[1]
    width = gain.shape[0]
    lines = spread.shape[1]
    return pl.pallas_call(
        mix_kernel,
        out_shape=(
            jax.ShapeDtypeStruct((rows, width), F32),
            jax.ShapeDtypeStruct((lines, width // Y), BF),
        ),
        name="mix_rows",
    )(parts, gain.reshape(1, width), spread)


def expert_kernel(in_hbm, up_hbm, down_hbm, out_ref, rows_ref, up_ref, down_ref, x_ref, sems):
    lines, col = rows_ref.shape
    pairs = lines // Y
    rows_copy = pltpu.make_async_copy(in_hbm, rows_ref, sems.at[0])
    gate_copy = pltpu.make_async_copy(up_hbm.at[0, 0], up_ref.at[0], sems.at[1])
    up_copy = pltpu.make_async_copy(up_hbm.at[0, 1], up_ref.at[1], sems.at[2])
    down_copy = pltpu.make_async_copy(down_hbm.at[0], down_ref, sems.at[3])
    rows_copy.start()
    gate_copy.start()
    up_copy.start()
    down_copy.start()

    target = lax.broadcasted_iota(jnp.int32, (lines, lines), 0)
    origin = lax.broadcasted_iota(jnp.int32, (lines, lines), 1)
    order = jnp.where(target % pairs * Y + target // pairs == origin, 1.0, 0.0).astype(BF)
    rows_copy.wait()
    sorted_rows = jnp.dot(order, rows_ref[...], preferred_element_type=F32).astype(BF)
    for t in range(Y):
        x_ref[:, t * col : (t + 1) * col] = sorted_rows[t * pairs : (t + 1) * pairs]
    gate_copy.wait()
    gate_val = jnp.dot(x_ref[...], up_ref[0], preferred_element_type=F32)
    up_copy.wait()
    upward = jnp.dot(x_ref[...], up_ref[1], preferred_element_type=F32)
    active = (gate_val / (1.0 + jnp.exp(-gate_val)) * upward).astype(BF)
    back = jnp.where(origin % pairs * Y + origin // pairs == target, 1.0, 0.0).astype(BF)
    down_copy.wait()
    tall = jnp.concatenate(
        [
            jnp.dot(
                active, down_ref[:, t * col : (t + 1) * col], preferred_element_type=F32
            ).astype(BF)
            for t in range(Y)
        ],
        axis=0,
    )
    out_ref[...] = jnp.dot(back, tall, preferred_element_type=F32).astype(BF)


def run_expert(inbound, gate_up, down):
    lines, col = inbound.shape
    _, _, width, hidden = gate_up.shape
    return pl.pallas_call(
        expert_kernel,
        in_specs=[pl.BlockSpec(memory_space=pl.ANY)] * 3,
        out_shape=jax.ShapeDtypeStruct((lines, col), BF),
        scratch_shapes=[
            pltpu.VMEM((lines, col), BF),
            pltpu.VMEM((2, width, hidden), BF),
            pltpu.VMEM((hidden, width), BF),
            pltpu.VMEM((lines // Y, width), BF),
            pltpu.SemaphoreType.DMA((4,)),
        ],
        name="run_expert",
    )(inbound, gate_up, down)


def on_device(
    queries,
    new_kv,
    residual,
    kv_cache,
    cache_len,
    request_perm,
    expert_ids,
    route_wt,
    attn_out_w,
    post_gain,
    expert_gate_up,
    expert_down,
    final_gain,
    vocab_w,
):
    vocab_other = lax.ppermute(vocab_w, "c", [(0, 1), (1, 0)])
    ix, iz, ic, iy = (lax.axis_index(a) for a in ALL)
    rows = queries.shape[0]
    groups = X * Z * C
    col = residual.shape[1]
    width = attn_out_w.shape[1]
    kv_width = new_kv.shape[2]
    head_dim = kv_width // 2
    cap = 2
    int_range = lambda n: jnp.arange(n, dtype=jnp.int32)

    packed = jnp.concatenate([queries, new_kv.reshape(rows, kv_width), residual], axis=1)
    plane = share(packed, ("x", "c"), X * C).reshape(X * C * rows, -1)
    plane_slots = lax.dynamic_index_in_dim(
        request_perm.reshape(X, Z, C * rows), iz, 1, keepdims=False
    ).reshape(-1)
    wanted_slots = (((ix * Z + int_range(Z)) * C + ic) * rows)[:, None] + int_range(rows)[None, :]
    select = (wanted_slots.reshape(-1)[:, None] == plane_slots[None, :]).astype(BF)
    outgoing = jnp.dot(select, plane, preferred_element_type=F32).astype(BF)
    arrived = lax.all_to_all(outgoing.reshape(Z, rows, -1), "z", 0, 0, tiled=True)
    mine = jnp.sum(arrived.astype(F32), axis=0).astype(BF)
    mine_q = mine[:, :col]
    mine_kv = mine[:, col : col + kv_width].reshape(rows, 1, kv_width)
    mine_res = mine[:, col + kv_width :]

    attended = attend(mine_q, mine_kv, kv_cache, cache_len, head_dim)
    partial_value = jnp.dot(attended, attn_out_w, preferred_element_type=F32).astype(BF)
    parts = share(jnp.concatenate([partial_value, mine_res], axis=1), "y", Y)
    spread, blend_two = route_tables(expert_ids, route_wt, groups, cap)
    lines = groups * cap * Y
    mixed_full, sent = mix_rows(parts, post_gain, spread)
    inbound = lax.all_to_all(sent.reshape(groups, cap * Y, col), REQ, 0, 0, tiled=True)
    produced = run_expert(inbound.reshape(lines, col), expert_gate_up, expert_down)

    returned = lax.all_to_all(
        produced.reshape(groups, cap * Y, col), REQ, 0, 0, tiled=True
    ).reshape(lines, col)
    moe_two = jnp.dot(blend_two.astype(BF), returned, preferred_element_type=F32)
    moe_part = (moe_two[: Y * rows] + moe_two[Y * rows :]).astype(BF)
    moe_part = jnp.concatenate([moe_part[t * rows : (t + 1) * rows] for t in range(Y)], axis=1)
    moe_full = jnp.sum(share(moe_part, "y", Y).astype(F32), axis=0)
    state = (mixed_full + moe_full).astype(BF)

    half = X * Z * rows
    every = share(share(state, ("z",), Z), ("x",), X).reshape(half, width)
    slot_of = ((int_range(X)[:, None] * Z + int_range(Z)[None, :]) * C + ic)[..., None]
    slot_of = (slot_of * rows + int_range(rows)).reshape(-1)
    gained = (every.astype(F32) * final_gain).astype(BF)
    meet = (((1,), (1,)), ((), ()))
    logits = lax.dot_general(gained, vocab_w, meet, preferred_element_type=F32)
    logits_other = lax.dot_general(gained, vocab_other, meet, preferred_element_type=F32)
    local_top = jnp.maximum(jnp.max(logits, axis=1), jnp.max(logits_other, axis=1))
    pick = request_perm[:, None] == slot_of[None, :]
    top_by_request = jnp.max(jnp.where(pick, local_top[None, :], -jnp.inf), axis=1)
    swap = [(0, 1), (1, 0)]
    every, top_by_request = lax.optimization_barrier((every, top_by_request))
    tops = jnp.broadcast_to(top_by_request.reshape(groups, 1, rows), (groups, Y, rows))
    tops = lax.all_to_all(tops.reshape(groups * Y, rows), ALL, 0, 0, tiled=True)

    chip_rows = C * rows
    wanted = lax.dynamic_slice_in_dim(request_perm, (ix * Z + iz) * chip_rows, chip_rows)
    back = wanted[:, None] == slot_of[None, :]
    found = jnp.dot(back.astype(BF), every, preferred_element_type=F32).astype(BF)
    crossed = lax.ppermute(
        jnp.where(ic == 0, found[rows:], found[:rows]), "c", swap
    )
    hidden = jnp.where(ic == 0, found[:rows], found[rows:]).astype(F32) + crossed.astype(F32)
    hidden_out = lax.dynamic_slice_in_dim(hidden, iy * col, col, 1).astype(BF)
    mean_eps = jnp.mean(hidden * hidden, axis=1) + epsilon
    top_logit = jnp.max(tops, axis=0) * lax.rsqrt(mean_eps)
    return (hidden_out, jnp.sqrt(mean_eps), top_logit)


def solution(mesh):
    fine = Mesh(mesh.devices.reshape(X, Z, C, Y), ALL)
    placed = (
        P(REQ, "y"),
        P(REQ, "y", None),
        P(REQ, "y"),
        P(REQ, None, "y", None),
        P(REQ),
        P(),
        P(REQ, None),
        P(REQ, None),
        P("y", None),
        P(),
        P(REQ, None, None, "y"),
        P(REQ, "y", None),
        P(),
        P(ALL, None),
    )
    return jax.shard_map(
        on_device,
        mesh=fine,
        in_specs=placed,
        out_specs=(P(REQ, "y"), P(REQ), P(REQ)),
        check_vma=False,
    )
```
